128 devices in a mesh: node: 32 (over x, y, core), local: 4 (over z).
Axes of the slice: x: 4, y: 4, z: 4, core: 2. Of those that a mesh axis runs over, the one named last changes fastest.
Arguments:
- expert_ids: int32 [16384, 4], P(('node', 'local')), may hold values from 0 to 127, as said below
- gate_weights: bfloat16 [16384, 4], P(('node', 'local')), may hold values from 0.099609375 to 1
- tokens_in: bfloat16 [16384, 3584], P(('node', 'local')), may hold values from -6 to 6
- grad_out: bfloat16 [16384, 3584], P(('node', 'local')), may hold values from -6 to 6
- w_gate: bfloat16 [128, 3584, 1024], P(('node', 'local')), may hold values from -0.09375 to 0.09375
- w_up: bfloat16 [128, 3584, 1024], P(('node', 'local')), may hold values from -0.09375 to 0.09375
- w_down: bfloat16 [128, 1024, 3584], P(('node', 'local')), may hold values from -0.1875 to 0.1875
Outputs:
- grad_in: bfloat16 [16384, 3584], P(('node', 'local'))
The draws below stay inside these ranges and needn't reach their ends.
Inputs may be any that keep to these rules, and one draw needn't show every extreme that they name: `expert_ids`: each token names 4 different experts, two in each of two different node groups; node group m holds experts 4 m to 4 m + 3. The tokens of one device pick every node group exactly 8 times. From the tokens of one device every expert gets at most 6 rows; in every node group one expert gets exactly 6 rows from every device, the others fewer, and every expert gets some rows.
All inputs are finite; a program needn't handle non-finite values.
Results may differ from the reference program's by a relative error of at most 0.0064.
Values may be sent and summed in bfloat16 or wider, within the bound.
A program may use at most 128 MiB of HBM per device.

```python
import jax
import jax.numpy as jnp
from jax import lax

D = 3584
FF = 1024
TOK_DEV = 128
TOP = 4
EXPERTS = 128
TOKENS = 16384
VISITS = 8
SLOTS = 6
N_NODE = 32
N_LOCAL = 4


def draw_expert_ids(key, part):
    blocks = TOKENS // TOK_DEV
    rounds = TOK_DEV // N_NODE
    key_perm, key_shift, key_visit, key_hot, key_order = jax.random.split(key, 5)
    perm_keys = jax.random.split(key_perm, blocks * rounds)
    node_perms = jax.vmap(lambda subkey: jax.random.permutation(subkey, N_NODE))(perm_keys)
    node_perms = node_perms.reshape(blocks, rounds, N_NODE).astype(jnp.int32)
    shifts = jax.random.randint(key_shift, (blocks, rounds, 1), 1, N_NODE).astype(jnp.int32)
    positions = jnp.arange(N_NODE, dtype=jnp.int32)
    node_first = node_perms.reshape(blocks, TOK_DEV)
    node_second = jnp.take_along_axis(node_perms, (positions[None, None, :] + shifts) % N_NODE, axis=2).reshape(blocks, TOK_DEV)
    picks = ((node_first[..., None] == positions) | (node_second[..., None] == positions)).astype(jnp.int32)
    before = jnp.cumsum(picks, axis=1) - picks
    visit_first = jnp.take_along_axis(before, node_first[..., None], axis=2)[..., 0]
    visit_second = jnp.take_along_axis(before, node_second[..., None], axis=2)[..., 0]
    visit_keys = jax.random.split(key_visit, blocks * N_NODE)
    visit_perms = jax.vmap(lambda subkey: jax.random.permutation(subkey, VISITS))(visit_keys)
    visit_perms = visit_perms.reshape(blocks, N_NODE * VISITS).astype(jnp.int32)
    pattern_first = jnp.take_along_axis(visit_perms, node_first * VISITS + visit_first, axis=1)
    pattern_second = jnp.take_along_axis(visit_perms, node_second * VISITS + visit_second, axis=1)
    hot_local = jax.random.randint(key_hot, (N_NODE,), 0, N_LOCAL).astype(jnp.int32)

    def choose(node_pick, pattern):
        hot_pick = hot_local[node_pick]
        step_mod = pattern % 3
        with_hot = pattern < 3 * VISITS // 4
        other_one = (hot_pick + 1 + step_mod) % N_LOCAL
        other_two = (hot_pick + 1 + (step_mod + 1) % 3) % N_LOCAL
        first_pick = jnp.where(with_hot, hot_pick, other_one)
        second_pick = jnp.where(with_hot, other_one, other_two)
        return (node_pick * N_LOCAL + first_pick, node_pick * N_LOCAL + second_pick)
    first_a, first_b = choose(node_first, pattern_first)
    second_a, second_b = choose(node_second, pattern_second)
    chosen = jnp.stack([first_a, first_b, second_a, second_b], axis=-1)
    scores = jax.random.randint(key_order, (blocks, TOK_DEV, TOP), 0, 1 << 20).astype(jnp.int32) * TOP + jnp.arange(TOP, dtype=jnp.int32)
    shuffle = jnp.argsort(scores, axis=-1)
    chosen = jnp.take_along_axis(chosen, shuffle, axis=-1)
    return chosen.reshape(TOKENS, TOP).astype(jnp.int32)


def block_levels(rng, shape, cuts, least, largest):
    loudness, own = 1.0, jax.random.fold_in(rng, 6)
    for axis_at, blocks in cuts:
        draws = jnp.exp(jax.random.uniform(jax.random.fold_in(own, axis_at), (blocks,), jnp.float32, least / len(cuts), largest / len(cuts)))
        loudness = loudness * jnp.repeat(draws, shape[axis_at] // blocks).reshape([-1 if axis == axis_at else 1 for axis in range(len(shape))])
    return loudness


def centred(stream_key, dims, spread, most, shards=(), kind=jnp.bfloat16):
    values = spread * jax.random.normal(stream_key, dims, jnp.float32)
    if shards:
        values = values * block_levels(stream_key, dims, shards, -0.22, 0.18)
    return jnp.clip(values, -most, most).astype(kind)


def setup_inputs(seed: int = 0) -> dict:
    key_of = jax.random.split(jax.random.key(seed), 8)
    return {
        "expert_ids": draw_expert_ids(jax.random.fold_in(key_of[7], 71), 0),
        "gate_weights": jnp.clip(0.099609375 + 0.9003906 * jax.random.uniform(key_of[1], (TOKENS, TOP), jnp.float32) ** block_levels(key_of[1], (TOKENS, TOP), ((0, 128),), -0.2, 0.2), 0.099609375, 1.0).astype(jnp.bfloat16),
        "tokens_in": centred(key_of[2], (TOKENS, D), 1.0, 6.0, ((0, 128),)),
        "grad_out": centred(key_of[3], (TOKENS, D), 1.0, 6.0, ((0, 128),)),
        "w_gate": centred(key_of[4], (EXPERTS, D, FF), D ** -0.5, 0.09375, ((0, 128),)),
        "w_up": centred(key_of[5], (EXPERTS, D, FF), D ** -0.5, 0.09375, ((0, 128),)),
        "w_down": centred(key_of[6], (EXPERTS, FF, D), FF ** -0.5, 0.1875, ((0, 128),)),
    }


def expert_rows(expert_x, expert_dy, gate_mat, up_mat, down_mat):
    pre_gate = jnp.dot(expert_x, gate_mat, preferred_element_type=jnp.float32)
    pre_up = jnp.dot(expert_x, up_mat, preferred_element_type=jnp.float32)
    grad_hidden = lax.dot_general(expert_dy, down_mat, (((1,), (1,)), ((), ())), preferred_element_type=jnp.float32)
    sigmoid_gate = jax.nn.sigmoid(pre_gate)
    grad_gate = (grad_hidden * pre_up * sigmoid_gate * (1.0 + pre_gate * (1.0 - sigmoid_gate))).astype(jnp.bfloat16)
    grad_up = (grad_hidden * pre_gate * sigmoid_gate).astype(jnp.bfloat16)
    summed = lax.dot_general(grad_gate, gate_mat, (((1,), (1,)), ((), ())), preferred_element_type=jnp.float32)
    summed = summed + lax.dot_general(grad_up, up_mat, (((1,), (1,)), ((), ())), preferred_element_type=jnp.float32)
    return summed.astype(jnp.bfloat16)


def buffer_rows(expert_ids):
    blocks = TOKENS // TOK_DEV
    grouped = expert_ids.reshape(blocks, TOK_DEV, TOP)
    onehot = jnp.sum((grouped[..., None] == jnp.arange(EXPERTS, dtype=jnp.int32)).astype(jnp.int32), axis=2)
    before = jnp.cumsum(onehot, axis=1) - onehot
    slot_rank = jnp.take_along_axis(before, grouped, axis=2).reshape(TOKENS, TOP)
    source = jnp.arange(TOKENS, dtype=jnp.int32) // TOK_DEV
    return (source[:, None] * SLOTS + slot_rank).astype(jnp.int32)


def reference(expert_ids, gate_weights, tokens_in, grad_out, w_gate, w_up, w_down):
    buffer_width = (TOKENS // TOK_DEV) * SLOTS
    flat_slot = (expert_ids * buffer_width + buffer_rows(expert_ids)).reshape(-1)
    token_numbers = jnp.repeat(jnp.arange(TOKENS, dtype=jnp.int32) + 1, TOP)
    token_of = jnp.zeros((EXPERTS * buffer_width,), jnp.int32).at[flat_slot].set(token_numbers)
    weight_of = jnp.zeros((EXPERTS * buffer_width,), jnp.float32).at[flat_slot].set(gate_weights.reshape(-1).astype(jnp.float32))
    token_of = token_of.reshape(EXPERTS, buffer_width)
    weight_of = weight_of.reshape(EXPERTS, buffer_width)

    def one_expert(carry, inputs):
        owner_row, weight, gate_mat, up_mat, down_mat = inputs
        present = owner_row > 0
        row_index = jnp.maximum(owner_row - 1, 0)
        expert_x = jnp.where(present[:, None], tokens_in[row_index], jnp.zeros((), jnp.bfloat16))
        expert_dy = (weight[:, None] * grad_out[row_index].astype(jnp.float32)).astype(jnp.bfloat16)
        row_grad = expert_rows(expert_x, expert_dy, gate_mat, up_mat, down_mat)
        target = jnp.where(present, row_index, TOKENS)
        carry = carry.at[target].add(row_grad.astype(jnp.float32), mode="drop")
        return carry, None

    start = jnp.zeros((TOKENS, D), jnp.float32)
    summed, unused = lax.scan(one_expert, start, (token_of, weight_of, w_gate, w_up, w_down))
    return summed.astype(jnp.bfloat16)
```

```python
import functools

import jax
import jax.numpy as jnp
from jax import lax
from jax.experimental import pallas as pl
from jax.experimental.pallas import tpu as pltpu
from jax.sharding import PartitionSpec as P

MESH = pl.DeviceIdType.MESH
F32 = jnp.float32
BF16 = jnp.bfloat16

NX, NY, NC, NZ = 4, 4, 2, 4
NODES = NX * NY * NC
TOK = 128
D = 3584
FF = 1024
HALF = D // 2
META = 128
W = D + META
CH = 4
PER = NODES // CH
HPER = PER // 2
FR = 16
SLOT = 6
ROWS = NZ * PER * SLOT
VIS = NZ * PER * FR


def dot(a, b):
    return jnp.dot(a, b, preferred_element_type=F32)


def dot_nt(a, b):
    return lax.dot_general(a, b, (((1,), (1,)), ((), ())), preferred_element_type=F32)


def steps_of(i):
    dx = (i // 2) % 4
    dy = (dx + i // 8) % 4
    return dx, dy, i % 2


def node_plus(node, i):
    dx, dy, dc = steps_of(i)
    return ((node // 8 + dx) % 4) * 8 + (((node // 2) % 4 + dy) % 4) * 2 + (node + dc) % 2


def node_minus(node, i):
    dx, dy, dc = steps_of(i)
    return ((node // 8 + 4 - dx) % 4) * 8 + (((node // 2) % 4 + 4 - dy) % 4) * 2 + (node + dc) % 2


def kernel(
    ids_ref, wts_ref, x_hbm, g_hbm, wg_hbm, wu_hbm, wd_hbm, out_ref,
    wg, wu, wd, frames, visits, xd, gg, gu, sel01, selw, onehot,
    part, ring1, ring2, back, got,
    load_sem, xs, xr, h1s, h1r, h2s, h2r, r1s, r1r, r2s, r2r, bs, br,
):
    node = lax.axis_index("node")
    local = lax.axis_index("local")
    up = (local + 1) % 4
    down = (local + 3) % 4

    loads = [
        pltpu.make_async_copy(x_hbm, xd.at[pl.ds(0, TOK)], load_sem.at[0]),
        pltpu.make_async_copy(g_hbm, xd.at[pl.ds(TOK, TOK)], load_sem.at[1]),
        pltpu.make_async_copy(wg_hbm, wg, load_sem.at[2]),
        pltpu.make_async_copy(wu_hbm, wu, load_sem.at[3]),
        pltpu.make_async_copy(wd_hbm, wd, load_sem.at[4]),
    ]
    for load in loads:
        load.start()

    barrier = pltpu.get_barrier_semaphore()

    @pl.loop(1, NODES)
    def _(i):
        pl.semaphore_signal(barrier, 1, device_id=(node_plus(node, i), local), device_id_type=MESH)

    for z in (up, down):
        pl.semaphore_signal(barrier, 1, device_id=(node, z), device_id_type=MESH)

    ids = ids_ref[...]
    wts = wts_ref[...]
    target = node_plus(node, lax.broadcasted_iota(jnp.int32, (NODES, TOK), 0))
    names = jnp.zeros((NODES, TOK), F32)
    weights = [jnp.zeros((NODES, TOK), F32) for _ in range(NZ)]
    for k in range(4):
        expert = ids[k : k + 1, :]
        names = jnp.where(expert // 4 == target, 1.0, names)
        for z in range(NZ):
            weights[z] = weights[z] + jnp.where(expert == target * 4 + z, wts[k : k + 1, :], 0.0)
    earlier = lax.broadcasted_iota(jnp.int32, (TOK, TOK), 0) < lax.broadcasted_iota(jnp.int32, (TOK, TOK), 1)
    rank = dot(names.astype(BF16), earlier.astype(F32).astype(BF16))
    rank = jnp.where(names > 0.5, rank, -1.0)
    shape = (NODES, FR, TOK)
    place = lax.broadcasted_iota(jnp.int32, shape, 1)
    chosen = rank[:, None, :] == (place % 8).astype(F32)
    low = place < 8
    one_x = jnp.where(chosen & low, 1.0, 0.0).reshape(NODES * FR, TOK)
    one_g = jnp.where(chosen & ~low, 1.0, 0.0).reshape(NODES * FR, TOK)
    onehot[:, pl.ds(0, TOK)] = one_x.astype(BF16)
    onehot[:, pl.ds(TOK, TOK)] = one_g.astype(BF16)
    lane = lax.broadcasted_iota(jnp.int32, shape, 2)
    meta = jnp.zeros(shape, F32)
    for z in range(NZ):
        value = jnp.sum(jnp.where(chosen, weights[z][:, None, :], 0.0), axis=2, keepdims=True)
        meta = jnp.where(lane == z, value, meta)
    frames[:, :, pl.ds(D, META)] = meta.astype(BF16)

    loads[0].wait()
    loads[1].wait()
    pl.semaphore_wait(barrier, NODES + 1)

    def send(i):
        return pltpu.make_async_remote_copy(
            frames.at[i], visits.at[0, i], xs.at[i], xr.at[i],
            device_id=(node_plus(node, i), local), device_id_type=MESH,
        )

    @pl.loop(0, CH)
    def _(c):
        row = pl.multiple_of(c * PER * FR, PER * FR)

        @pl.loop(0, D // 512)
        def _(t):
            col = pl.multiple_of(t * 512, 512)
            block = dot(onehot[pl.ds(row, PER * FR), :], xd[pl.ds(0, 2 * TOK), pl.ds(col, 512)])
            frames[pl.ds(c * PER, PER), :, pl.ds(col, 512)] = block.astype(BF16).reshape(PER, FR, 512)

        @pl.loop(0, PER)
        def _(k):
            @pl.when(c * PER + k > 0)
            def _():
                send(c * PER + k).start()

    visits[0, 0] = frames[0]

    def hop1(c, way):
        peer, slot = ((up, 1), (down, 3))[way]
        return pltpu.make_async_remote_copy(
            visits.at[0, pl.ds(c * PER, PER)], visits.at[slot, pl.ds(c * PER, PER)],
            h1s.at[way, c], h1r.at[way, c], device_id=(node, peer), device_id_type=MESH,
        )

    def hop2(c, way):
        peer, slot = ((up, 1), (down, 3))[way]
        part_of = pl.ds(c * PER + way * HPER, HPER)
        return pltpu.make_async_remote_copy(
            visits.at[slot, part_of], visits.at[2, part_of],
            h2s.at[way, c], h2r.at[way, c], device_id=(node, peer), device_id_type=MESH,
        )

    def sum1(c, way):
        peer = (down, up)[way]
        return pltpu.make_async_remote_copy(
            part.at[c % 2, 2, pl.ds(way * HPER, HPER)], ring1.at[way, c],
            r1s.at[way, c], r1r.at[way, c], device_id=(node, peer), device_id_type=MESH,
        )

    def sum2(c, way):
        peer, slot = ((down, 1), (up, 3))[way]
        return pltpu.make_async_remote_copy(
            part.at[c % 2, slot], ring2.at[way, c],
            r2s.at[way, c], r2r.at[way, c], device_id=(node, peer), device_id_type=MESH,
        )

    def give(i):
        return pltpu.make_async_remote_copy(
            back.at[i], got.at[i], bs.at[i], br.at[i],
            device_id=(node_minus(node, i), local), device_id_type=MESH,
        )

    def select(c):
        info = visits[:, pl.ds(c * PER, PER), :, pl.ds(D, META)].reshape(VIS, META).astype(F32)
        lanes = lax.broadcasted_iota(jnp.int32, (VIS, META), 1)
        weight = jnp.sum(jnp.where(lanes == local, info, 0.0), axis=1, keepdims=True)
        mine = jnp.where(weight > 0.0, 1.0, 0.0)
        wide = jnp.broadcast_to(mine, (VIS, META)).astype(BF16)
        r = lax.broadcasted_iota(jnp.int32, (128, 128), 0)
        q = lax.broadcasted_iota(jnp.int32, (128, 128), 1)
        tri = jnp.where((r // 8 == q // 8) & (q < r), 1.0, 0.0).astype(BF16)
        ranks = jnp.concatenate(
            [dot(tri, wide[b * 128 : (b + 1) * 128]) for b in range(VIS // 128)], axis=0
        )
        ranks = jnp.where(mine > 0.5, ranks, -1.0)
        ranks = jnp.concatenate([ranks] * (2 * ROWS // META), axis=1)
        rr = lax.broadcasted_iota(jnp.int32, (VIS, 2 * ROWS), 0)
        cc = lax.broadcasted_iota(jnp.int32, (VIS, 2 * ROWS), 1)
        second = jnp.where(cc >= ROWS, 1, 0)
        cc = cc - ROWS * second
        frame = (cc * 171) >> 10
        slot = cc - 6 * frame
        hit = (ranks == slot.astype(F32)) & (rr // 8 == 2 * frame + second)
        ones = jnp.where(hit, 1.0, 0.0)
        sel01[...] = ones.astype(BF16)
        scaled = jnp.where(second == 1, ones * weight, ones)
        selw[...] = jnp.transpose(scaled).astype(BF16)

    def compute(c):
        select(c)

        @pl.loop(0, D // 512)
        def _(t):
            col = pl.multiple_of(t * 512, 512)
            block = visits[:, pl.ds(c * PER, PER), :, pl.ds(col, 512)].reshape(VIS, 512)
            xd[:, pl.ds(col, 512)] = dot(selw[...], block).astype(BF16)

        @pl.loop(0, FF // 256)
        def _(t):
            col = pl.multiple_of(t * 256, 256)
            pre_gate = dot(xd[pl.ds(0, ROWS), :], wg[:, pl.ds(col, 256)])
            pre_up = dot(xd[pl.ds(0, ROWS), :], wu[:, pl.ds(col, 256)])
            grad_hidden = dot_nt(xd[pl.ds(ROWS, ROWS), :], wd[pl.ds(col, 256), :])
            sig = 1.0 / (1.0 + jnp.exp(-pre_gate))
            gg[:, pl.ds(col, 256)] = (grad_hidden * pre_up * sig * (1.0 + pre_gate * (1.0 - sig))).astype(BF16)
            gu[:, pl.ds(col, 256)] = (grad_hidden * pre_gate * sig).astype(BF16)

        @pl.loop(0, HALF // 256)
        def _(t):
            col = pl.multiple_of(t * 256, 256)
            pieces = []
            for h in range(2):
                at = pl.ds(pl.multiple_of(h * HALF + t * 256, 256), 256)
                pieces.append((dot_nt(gg[...], wg[at, :]) + dot_nt(gu[...], wu[at, :])).astype(BF16))
            rows = jnp.concatenate(pieces, axis=0)
            block = dot(sel01[...], rows).astype(BF16)
            part[c % 2, :, :, :, pl.ds(col, 256)] = block.reshape(NZ, PER, FR, 256)

    @pl.loop(0, CH + 4)
    def _(s):
        @pl.when(s < CH)
        def _():
            @pl.loop(0, PER)
            def _(k):
                @pl.when(s * PER + k > 0)
                def _():
                    send(s * PER + k).wait_recv()

            hop1(s, 0).start()
            hop1(s, 1).start()

        @pl.when((s >= 1) & (s <= CH))
        def _():
            for way in range(2):
                hop1(s - 1, way).wait_recv()
                hop2(s - 1, way).start()

        @pl.when((s >= 3) & (s <= CH + 2))
        def _():
            c = s - 3
            for way in range(2):
                sum1(c, way).wait_recv()
                slot = (1, 3)[way]
                at = pl.ds(way * HPER, HPER)
                both = part[c % 2, slot, at].astype(F32) + ring1[way, c].astype(F32)
                part[c % 2, slot, at] = both.astype(BF16)
                sum2(c, way).start()

        @pl.when(s == 2)
        def _():
            for load in loads[2:]:
                load.wait()

        @pl.when(s >= 4)
        def _():
            c = s - 4
            for way in range(2):
                sum2(c, way).wait_recv()
            base = c * PER

            @pl.loop(0, PER)
            def _(k):
                total = part[c % 2, 0, k].astype(F32) + ring2[0, c, k].astype(F32) + ring2[1, c, k].astype(F32)
                back[base + k] = total.astype(BF16)

                @pl.when(base + k > 0)
                def _():
                    give(base + k).start()

        @pl.when((s >= 2) & (s <= CH + 1))
        def _():
            c = s - 2
            for way in range(2):
                hop2(c, way).wait_recv()

            @pl.when(c >= 2)
            def _():
                for way in range(2):
                    sum1(c - 2, way).wait_send()
                    sum2(c - 2, way).wait_send()

            compute(c)
            for way in range(2):
                sum1(c, way).start()

    got[0] = back[0]

    @pl.loop(1, NODES)
    def _(i):
        give(i).wait_recv()

    @pl.loop(0, HALF // 256)
    def _(t):
        col = pl.multiple_of(t * 256, 256)
        block = got[:, :, pl.ds(col, 256)].reshape(NODES * FR, 256)
        total = lax.dot_general(
            onehot[...], block, (((0,), (0,)), ((), ())), preferred_element_type=F32
        )
        out_ref[:, pl.ds(col, 256)] = total[:TOK].astype(BF16)
        out_ref[:, pl.ds(pl.multiple_of(HALF + t * 256, 256), 256)] = total[TOK:].astype(BF16)

    @pl.loop(1, NODES)
    def _(i):
        send(i).wait_send()
        give(i).wait_send()

    @pl.loop(0, CH)
    def _(c):
        for way in range(2):
            hop1(c, way).wait_send()
            hop2(c, way).wait_send()

    for c in range(CH - 2, CH):
        for way in range(2):
            sum1(c, way).wait_send()
            sum2(c, way).wait_send()


def per_device(expert_ids, gate_weights, tokens_in, grad_out, w_gate, w_up, w_down):
    ids = jnp.pad(expert_ids.T, ((0, 4), (0, 0)), constant_values=-1)
    wts = jnp.pad(gate_weights.astype(F32).T, ((0, 4), (0, 0)))
    vmem = pl.BlockSpec(memory_space=pltpu.VMEM)
    hbm = pl.BlockSpec(memory_space=pl.ANY)
    dma = pltpu.SemaphoreType.DMA
    return pl.pallas_call(
        kernel,
        out_shape=jax.ShapeDtypeStruct((TOK, D), BF16),
        in_specs=[vmem, vmem, hbm, hbm, hbm, hbm, hbm],
        out_specs=vmem,
        scratch_shapes=[
            pltpu.VMEM((D, FF), BF16),
            pltpu.VMEM((D, FF), BF16),
            pltpu.VMEM((FF, D), BF16),
            pltpu.VMEM((NODES, FR, W), BF16),
            pltpu.VMEM((NZ, NODES, FR, W), BF16),
            pltpu.VMEM((2 * ROWS, D), BF16),
            pltpu.VMEM((ROWS, FF), BF16),
            pltpu.VMEM((ROWS, FF), BF16),
            pltpu.VMEM((VIS, 2 * ROWS), BF16),
            pltpu.VMEM((2 * ROWS, VIS), BF16),
            pltpu.VMEM((NODES * FR, 2 * TOK), BF16),
            pltpu.VMEM((2, NZ, PER, FR, HALF), BF16),
            pltpu.VMEM((2, CH, HPER, FR, HALF), BF16),
            pltpu.VMEM((2, CH, PER, FR, HALF), BF16),
            pltpu.VMEM((NODES, FR, HALF), BF16),
            pltpu.VMEM((NODES, FR, HALF), BF16),
            dma((5,)),
            dma((NODES,)), dma((NODES,)),
            dma((2, CH)), dma((2, CH)), dma((2, CH)), dma((2, CH)),
            dma((2, CH)), dma((2, CH)), dma((2, CH)), dma((2, CH)),
            dma((NODES,)), dma((NODES,)),
        ],
        compiler_params=pltpu.CompilerParams(
            collective_id=0, has_side_effects=True, vmem_limit_bytes=65 * 1024 * 1024
        ),
    )(ids, wts, tokens_in, grad_out, w_gate[0], w_up[0], w_down[0])


def solution(mesh):
    placed = (
        P(("node", "local"), None),
        P(("node", "local"), None),
        P(("node", "local"), None),
        P(("node", "local"), None),
        P(("node", "local"), None, None),
        P(("node", "local"), None, None),
        P(("node", "local"), None, None),
    )
    return jax.shard_map(
        per_device,
        mesh=mesh,
        in_specs=placed,
        out_specs=P(("node", "local"), None),
        check_vma=False,
    )
```
